32 devices in a mesh: row: 4 (over y, x), col: 8 (over z, core).
Axes of the slice: x: 2, y: 2, z: 4, core: 2. Of those that a mesh axis runs over, the one named last changes fastest.
Arguments:
- amplitudes: bfloat16 [4096, 16384], P('col', 'row'), may hold values from -6 to 6
- integrals: bfloat16 [4096, 16384], P('row', 'col'), may hold values from -0.09375 to 0.09375
- tile_mask: int32 [64, 256], P(None, 'row'), may hold values from 0 to 1, as said below
- occ_energy: float32 [4], replicated, may hold values from -1 to -0.2
- virt_energy: float32 [4096], replicated, may hold values from 0.2 to 1.5
Outputs:
- update: bfloat16 [16384, 16384], P(('row', 'col'))
The draws below stay inside these ranges and needn't reach their ends.
Inputs may be any that keep to these rules, and one draw needn't show every extreme that they name: `tile_mask`: 0 drops a tile, 1 keeps it; the share of kept tiles differs strongly between groups of (ia) rows.
All inputs are finite; a program needn't handle non-finite values.
Results may differ from the reference program's by a relative error of at most 0.0049.
Values may be sent and summed in bfloat16 or wider, within the bound.
A program may use at most 192 MiB of HBM per device.

```python
import jax
import jax.numpy as jnp
from jax import lax

V = 4096
TILE = 64
NI = 4
KW = 4096
M = 16384
N_ROW = 4
N_COL = 8


def draw_tile_mask(key, part):
    tile_depth = KW // TILE
    tile_width = M // TILE
    groups = N_ROW
    depth_blocks = N_COL
    first_key, second_key = jax.random.split(jax.random.fold_in(key, 7))
    levels = jax.random.randint(first_key, (depth_blocks, groups), 0, 100)
    bounds = 20 + 70 * jnp.arange(groups, dtype=jnp.int32) // max(groups - 1, 1)
    active = (levels < bounds[None, :]).astype(jnp.int32)
    active = jnp.repeat(jnp.repeat(active, tile_depth // depth_blocks, axis=0), tile_width // groups, axis=1)
    tiles = (jax.random.randint(second_key, (tile_depth, tile_width), 0, 4) > 0).astype(jnp.int32)
    return active * tiles


def block_scale(rng, shape, cuts, least, top_value):
    loudness = 1.0
    for dim, parts in cuts:
        steps = jax.random.uniform(jax.random.fold_in(jax.random.fold_in(rng, 6), dim), (parts,), jnp.float32, least / len(cuts), top_value / len(cuts))
        loudness = loudness * jnp.repeat(jnp.exp(steps), shape[dim] // parts).reshape((-1,) + (1,) * (len(shape) - 1 - dim))
    return loudness


def noise(rng, extent, spread, most, pieces=(), kind=jnp.bfloat16):
    level = block_scale(rng, extent, pieces, -0.22, 0.18) if pieces else 1.0
    values = jax.random.normal(rng, extent, jnp.float32) * spread * level
    return jnp.minimum(jnp.maximum(values, -most), most).astype(kind)


def setup_inputs(seed: int = 0) -> dict:
    key_list = jax.random.split(jax.random.key(seed), 6)
    return {
        "amplitudes": noise(key_list[0], (KW, M), 1.0, 6.0, ((0, 8), (1, 4))),
        "integrals": noise(key_list[1], (KW, M), KW ** -0.5, 0.09375, ((0, 4), (1, 8))),
        "tile_mask": draw_tile_mask(jax.random.fold_in(key_list[5], 71), 0),
        "occ_energy": jnp.clip(jax.random.uniform(key_list[3], (NI,), jnp.float32, -1.0, -0.2), -1.0, -0.2),
        "virt_energy": jnp.clip(jax.random.uniform(key_list[4], (V,), jnp.float32, 0.2, 1.5), 0.2, 1.5),
    }


def reference(amplitudes, integrals, tile_mask, occ_energy, virt_energy):
    tile_depth, tile_width = tile_mask.shape
    keep_tiles = tile_mask.astype(jnp.bfloat16)
    masked = (amplitudes.reshape(tile_depth, TILE, tile_width, TILE) * keep_tiles[:, None, :, None]).reshape(KW, M)
    cycle_block = jnp.dot(masked.T, integrals, preferred_element_type=jnp.float32).astype(jnp.bfloat16)
    pair_gap = (virt_energy[None, :] - occ_energy[:, None]).astype(jnp.float32).reshape(M)
    block_rows = min(M, 1024)

    def mirror_block(index_block):
        offset = index_block * block_rows
        row_block = lax.dynamic_slice_in_dim(cycle_block, offset, block_rows, 0).astype(jnp.float32)
        col_block = lax.dynamic_slice_in_dim(cycle_block, offset, block_rows, 1).astype(jnp.float32).T
        gap_block = lax.dynamic_slice_in_dim(pair_gap, offset, block_rows, 0)
        return ((row_block + col_block) / (gap_block[:, None] + pair_gap[None, :])).astype(jnp.bfloat16)

    result = lax.map(mirror_block, jnp.arange(M // block_rows, dtype=jnp.int32))
    return result.reshape(M, M)
```

```python
import functools

import jax
import jax.numpy as jnp
from jax import lax
from jax.experimental import pallas as pl
from jax.experimental.pallas import tpu as pltpu
from jax.sharding import PartitionSpec as P

TILE = 64
MESH = pl.DeviceIdType.MESH
VMEM_BYTES = 66_000_000
DIMS = (((0,), (0,)), ((), ()))


def xor(u, v, n):
    total, bit = 0, 1
    while bit < n:
        total = total + (((u // bit) % 2 + (v // bit) % 2) % 2) * bit
        bit *= 2
    return total


def bits_of(n):
    out, bit = [], 1
    while bit < n:
        out.append(bit)
        bit *= 2
    return out


def children(m, parity, n):
    if m == 0:
        return bits_of(n)
    have = [b for b in bits_of(n) if m & b]
    if parity == 0:
        return [b for b in bits_of(n) if b < have[0]]
    return [b for b in bits_of(n) if b > have[-1]]


def after(k, n):
    odd = k % 2 == 1
    up = jnp.where(k + 2 <= n - 1, k + 2, n - 2)
    down = jnp.where(k == 0, 1, k - 2)
    return jnp.where(odd, up, down)


def before(k, n):
    odd = k % 2 == 1
    up = jnp.where(k + 2 <= n - 2, k + 2, n - 1)
    down = jnp.where(k == 1, 0, k - 2)
    return jnp.where(odd, down, up)


def kernel(
    nr, nc, a_ref, b_ref, rg_ref, cg_ref, out, a_full, ib,
    ra, rb, ca, cb, stage, twin,
    s_own, s_fwd, s_part, s_ra, s_rb, s_bc, s_hand, s_rra, s_rrb, s_po, s_out, s_tw,
    q_a, q_g, q_q, q_ra, q_rb, q_out, l_c, l_r,
):
    r = lax.axis_index("row")
    c = lax.axis_index("col")
    n = nc // 2
    k = c // 2
    p = c % 2
    partner = c + 1 - 2 * p
    d, w = a_ref.shape
    e = b_ref.shape[0]
    sub = w // n
    q = sub // 2
    half = n // 2
    depth = d * nc
    nxt, prv = after(k, n), before(k, n)
    low = k < half
    top_skip = (n - 1) - 2 if n > 2 else 0
    bottom_skip = 2
    bits = bits_of(nr)

    barrier = pltpu.get_barrier_semaphore()

    def greet(row, col):
        pl.semaphore_signal(barrier, inc=1, device_id=(row, col), device_id_type=MESH)

    greet(r, partner)
    for m in range(1, nr):
        greet(xor(r, m, nr), c)
        greet(xor(r, m, nr), partner)
    greet(r, (c + 2) % nc)
    greet(r, (c - 2 + nc) % nc)
    for t in range(2):
        greet(r, 2 * nxt + t)
        greet(r, 2 * prv + t)
    pl.semaphore_wait(barrier, 1 + 2 * (nr - 1) + 2 + 4)

    state = {"wait": False}

    def run(cond, body):
        if cond is None:
            body()
        else:
            pl.when(cond)(body)

    def both(*conds):
        total = None
        for x in conds:
            if x is None:
                continue
            total = x if total is None else jnp.logical_and(total, x)
        return total

    def no(x):
        return jnp.logical_not(x)

    def send(src, dst, sem, recv, row, col, cond=None):
        copy = pltpu.make_async_remote_copy(
            src_ref=src, dst_ref=dst, send_sem=sem, recv_sem=recv,
            device_id=(row, col), device_id_type=MESH,
        )
        run(cond, copy.wait_send if state["wait"] else copy.start)

    def local(src, dst, sem, cond=None):
        if not state["wait"]:
            run(cond, pltpu.make_async_copy(src, dst, sem).start)

    def arrived(ref, sem, cond=None):
        if not state["wait"]:
            run(cond, pltpu.make_async_copy(ref, ref, sem).wait)

    def ds(start, size):
        return pl.ds(pl.multiple_of(start, size), size)

    def a_rows(col):
        return ds(col * d, d)

    def b_rows(row):
        return ds(row * e, e)

    def cols(kp):
        return ds(kp * sub, sub)

    def raw(kk, kp, plane):
        direct = jnp.logical_and(kk == r, kp != plane)
        return b_rows(jnp.where(direct, r, nr + kk))

    own = ds(c * q, q)

    def rows_a(src, col, cond):
        for x, b in enumerate(bits):
            send(src, ra.at[b, a_rows(col), :], s_ra.at[col, x], q_ra.at[b, col], xor(r, b, nr), c, cond)

    def b_out(src, kk, kp, cond, mine):
        is_row = both(cond, kp == k)
        for t in range(2):
            part = src.at[:, pl.ds(t * q, q)]
            for x, b in enumerate(bits):
                row = xor(r, b, nr)
                send(part, rb.at[xor(row, kk, nr), b_rows(r), :], s_rb.at[kk, t, x], q_rb.at[b, kk], row, 2 * k + t, is_row)
            dst = rb.at[xor(r, kk, nr), b_rows(r), :]
            local(part, dst, q_rb.at[0, kk], both(is_row, p == t))
            send(part, dst, s_rb.at[kk, t, len(bits)], q_rb.at[0, kk], r, partner, both(is_row, p != t))
        is_col = both(cond, kp != k, kp != prv)
        dst = ib.at[b_rows(r), cols(kp)]
        send(src, dst, s_bc.at[kk, kp], q_q.at[r, kp], kk, c, both(is_col, kk != r))
        send(src, dst, s_bc.at[kk, kp], q_q.at[r, kp], r, partner, both(is_col, kk == r))
        if mine:
            local(src, dst, q_q.at[r, kp], both(is_col, kk == r))

    def blocked(target, kp):
        return jnp.logical_or(
            jnp.logical_and(target == 0, kp == bottom_skip),
            jnp.logical_and(target == n - 1, kp == top_skip),
        )

    def owner(kp):
        return kp // half == p

    def piece(sign, j):
        return n - 1 - j if sign > 0 else j

    def valid(j):
        return jnp.logical_and(j >= 0, j < n)

    def clip(x, top):
        return jnp.clip(x, 0, top)

    def issue_own(sign, j, least=0):
        ok = jnp.logical_and(j >= least, j < n)
        kp = piece(sign, clip(j, n - 1))
        far = k + sign
        ok = both(ok, far >= 0, far < n, no(blocked(far, kp)))
        x = 0 if sign > 0 else 1
        target = clip(c + 2 * sign, nc - 1)
        send(a_ref.at[:, cols(kp)], a_full.at[a_rows(c), cols(kp)], s_own.at[x, 0, kp], q_a.at[c, kp], r, target, ok)
        send(
            b_ref.at[:, cols(kp % half)], ib.at[raw(k, kp, far), cols(kp)], s_own.at[x, 1, kp], q_g.at[k, kp],
            r, target, both(ok, owner(kp)),
        )

    def relay(sign, j, s):
        kp = piece(sign, clip(j, n - 1))
        src = k - sign * s
        here = both(valid(j), src >= 0, src < n, no(blocked(k, kp)))
        kk = clip(src, n - 1)
        far = k + sign
        onward = both(here, far >= 0, far < n, no(blocked(far, kp)))
        x = 0 if sign > 0 else 1
        target = clip(c + 2 * sign, nc - 1)
        col = 2 * kk + p
        a_piece = a_full.at[a_rows(col), cols(kp)]
        arrived(a_piece, q_a.at[col, kp], here)
        send(a_piece, a_piece, s_fwd.at[x, s - 1, 0, kp], q_a.at[col, kp], r, target, onward)
        send(a_piece, a_piece, s_part.at[kk, kp], q_a.at[col, kp], r, partner, both(here, kp != prv))
        rows_a(a_full.at[a_rows(col), own], col, both(here, kp == k))
        mine = both(here, owner(kp))
        b_piece = ib.at[raw(kk, kp, k), cols(kp)]
        arrived(b_piece, q_g.at[kk, kp], mine)
        send(
            b_piece, ib.at[raw(kk, kp, far), cols(kp)], s_fwd.at[x, s - 1, 1, kp], q_g.at[kk, kp],
            r, target, both(onward, owner(kp)),
        )
        b_out(b_piece, kk, kp, mine, False)

    def partner_rows(kk, cond):
        col = 2 * kk + 1 - p
        ref = a_full.at[a_rows(col), cols(k)]
        arrived(ref, q_a.at[col, k], cond)
        rows_a(a_full.at[a_rows(col), own], col, cond)

    def own_part():
        rows_a(a_ref.at[:, own], c, None)

        @pl.loop(0, n)
        def _(kp):
            b_out(b_ref.at[:, cols(kp % half)], k, kp, owner(kp), True)
            part = a_ref.at[:, cols(kp)]
            dst = a_full.at[a_rows(c), cols(kp)]
            send(part, dst, s_part.at[k, kp], q_a.at[c, kp], r, partner, kp != prv)
            local(part, dst, q_a.at[c, kp], kp != prv)

    def slot(tau):
        up = tau + jnp.where(low, 1, 0)
        down = tau + jnp.where(low, 0, 1)
        issue_own(1, up + 1, 1)
        issue_own(-1, down + 1, 1)
        for s in range(1, n):
            relay(1, up, s)
            relay(-1, down, s)
        for s in range(1, n):
            for sign, j in ((1, up), (-1, down)):
                src = k - sign * s
                cond = both(valid(j), src >= 0, src < n, piece(sign, j) == k)
                partner_rows(clip(src, n - 1), cond)

    mirrored = jnp.where(low, k, n - 1 - k)
    ready = jnp.where(mirrored == 0, 0, jnp.maximum(mirrored, n - 2 - mirrored))

    def relay_rows():
        for m in range(nr):
            origin = xor(r, m, nr)

            @pl.loop(0, n)
            def _(kk, m=m, origin=origin):
                for pp in range(2):
                    col = 2 * kk + pp
                    if m:
                        got = ra.at[m, a_rows(col), :]
                        arrived(got, q_ra.at[m, col])
                        for b in children(m, pp, nr):
                            x = bits.index(b)
                            send(got, ra.at[m | b, a_rows(col), :], s_rra.at[col, m, x], q_ra.at[m | b, col], xor(r, b, nr), c)

            @pl.loop(0, half)
            def _(gg, m=m, origin=origin):
                for pg in range(2):
                    g = 2 * gg + pg
                    got = rb.at[xor(r, g, nr), b_rows(origin), :]
                    arrived(got, q_rb.at[m, g])
                    if m:
                        for b in children(m, pg, nr):
                            x = bits.index(b)
                            row = xor(r, b, nr)
                            send(
                                got, rb.at[xor(row, g, nr), b_rows(origin), :], s_rrb.at[g, m, x],
                                q_rb.at[m | b, g], row, c,
                            )
                    send(
                        got, ib.at[b_rows(origin), own], s_po.at[m], q_q.at[origin, k], r, partner, g == r,
                    )

    def hand(kp, cond):
        mine = both(cond, owner(kp))
        for m in range(nr):
            row = xor(r, m, nr)
            ref = ib.at[b_rows(row), cols(kp)]
            if m:
                arrived(ref, q_q.at[row, kp], mine)
                send(ref, ref, s_hand.at[row, kp], q_q.at[row, kp], r, partner, mine)
            else:
                arrived(ref, q_q.at[row, kp], both(mine, k == r))

    def tile_piece(t):
        rank = jnp.where(low, prv, n - 1 - prv)
        base = jnp.where(mirrored < rank, mirrored, mirrored - 1)
        i = jnp.where(t == 0, base, jnp.where(t <= base, t - 1, t))
        i = jnp.where(i >= rank, i + 1, i)
        return jnp.where(low, i, n - 1 - i)

    def tile(t):
        kp = tile_piece(t)
        is_own = kp == k
        for kk in range(n):
            col = 2 * kk + 1 - p
            arrived(a_full.at[a_rows(col), cols(kp)], q_a.at[col, kp], no(is_own))
        arrived(a_full.at[a_rows(c), cols(kp)], q_a.at[c, kp], no(is_own))
        for row in range(nr):
            arrived(ib.at[b_rows(row), cols(kp)], q_q.at[row, kp], both(no(is_own), no(owner(kp))))
            arrived(ib.at[b_rows(row), own], q_q.at[row, k], is_own)

        def load(h):
            where = ds((2 * kp + h) * q, q)
            full = pl.ds(0, depth)
            pltpu.make_async_copy(a_full.at[:, where], ca.at[h], l_c.at[h, 0]).start()
            mine = jnp.logical_and(is_own, p == h)
            run(mine, pltpu.make_async_copy(rb.at[0], cb.at[h], l_c.at[h, 1]).start)
            run(no(mine), pltpu.make_async_copy(ib.at[full, where], cb.at[h], l_c.at[h, 1]).start)

        for h in range(2):
            load(h)

        @pl.loop(0, 2)
        def _(h):
            where = ds((2 * kp + h) * q, q)
            pltpu.make_async_copy(ca.at[h], ca.at[h], l_c.at[h, 0]).wait()
            pltpu.make_async_copy(cb.at[h], cb.at[h], l_c.at[h, 1]).wait()

            @pl.loop(0, nr)
            def _(i):
                m = nr - 1 - i
                row = xor(r, m, nr)
                buf = stage.at[h, m]
                run(t > 0, pltpu.make_async_copy(buf, buf, s_out.at[h, m]).wait)
                total = lax.dot_general(ra[m], cb[h], DIMS, preferred_element_type=jnp.float32)
                total += lax.dot_general(rb[m], ca[h], DIMS, preferred_element_type=jnp.float32)
                total = total / (rg_ref[m] + cg_ref[:, where])
                stage[h, m] = total.astype(stage.dtype)
                dst = out.at[:, ds(r * w + (2 * kp + h) * q, q)]
                remote = pltpu.make_async_remote_copy(
                    src_ref=buf, dst_ref=dst, send_sem=s_out.at[h, m], recv_sem=q_out,
                    device_id=(row, c), device_id_type=MESH,
                )
                run(m > 0, remote.start)
                run(m == 0, pltpu.make_async_copy(buf, dst, s_out.at[h, m]).start)

                @pl.when(kp == nxt)
                def _():
                    twin[h, m] = total.T.astype(twin.dtype)
                    pltpu.make_async_remote_copy(
                        src_ref=twin.at[h, m], dst_ref=out.at[:, ds(row * w + c * q, q)],
                        send_sem=s_tw.at[h, m], recv_sem=q_out,
                        device_id=(r, 2 * kp + h), device_id_type=MESH,
                    ).start()

    end = mirrored == 0

    def start():
        for sign in (1, -1):
            issue_own(sign, jnp.int32(0))
        own_part()
        partner_rows(k, None)

    start()

    @pl.loop(0, n + 1)
    def _(x):
        slot(x - 2)
        pl.when(x - 2 == ready)(relay_rows)

    arrived(a_full.at[a_rows(c), cols(k)], q_a.at[c, k])
    load_own = pltpu.make_async_copy(a_full.at[:, own], ra.at[0], l_r)
    load_own.start()
    load_own.wait()
    hand(tile_piece(1), None)

    @pl.loop(0, n)
    def _(x):
        last = x == jnp.where(end, 2, 1)

        @pl.when(last)
        def _():
            slot(x * 0 + n - 1)
            hand(tile_piece(2), None)

        @pl.when(no(last))
        def _():
            t = jnp.where(x == 0, 0, jnp.where(x > 2, x - 1, 1))
            more = jnp.logical_and(x > 2, x < n - 1)
            hand(tile_piece(jnp.where(more, x, 1)), more)
            tile(t)

    state["wait"] = True
    start()

    @pl.loop(0, n + 2)
    def _(x):
        slot(x - 2)

    relay_rows()

    @pl.loop(1, n - 1)
    def _(t):
        hand(tile_piece(t), None)

    @pl.loop(0, 2)
    def _(h):
        @pl.loop(0, nr)
        def _(m):
            pltpu.make_async_copy(stage.at[h, m], stage.at[h, m], s_out.at[h, m]).wait()
            pltpu.make_async_copy(twin.at[h, m], twin.at[h, m], s_tw.at[h, m]).wait()

    landed = out.at[:, pl.ds(0, (nr - 1) * (n - 1) * sub + nr * sub)]
    pltpu.make_async_copy(landed, landed, q_out).wait()


def fused(nr, nc, a, b, row_gap, col_gap):
    d, w = a.shape
    e = b.shape[0]
    n = nc // 2
    depth = d * nc
    q = w // nc
    nb = len(bits_of(nr))
    dma = pltpu.SemaphoreType.DMA
    hbm = pl.BlockSpec(memory_space=pl.ANY)
    vmem = pl.BlockSpec(memory_space=pltpu.VMEM)
    shapes = [(q, nr * w), (depth, w), ((nr + n) * e, w)]
    block = pltpu.VMEM((nr, depth, q), a.dtype)
    pair = pltpu.VMEM((2, depth, q), a.dtype)
    tiles = pltpu.VMEM((2, nr, q, q), a.dtype)
    return pl.pallas_call(
        functools.partial(kernel, nr, nc),
        out_shape=[jax.ShapeDtypeStruct(s, a.dtype) for s in shapes],
        in_specs=[hbm, hbm, vmem, vmem],
        out_specs=[hbm] * 3,
        scratch_shapes=[
            block, block, pair, pair, tiles, tiles,
            dma((2, 2, n)), dma((2, n - 1, 2, n)), dma((n, n)), dma((nc, nb)), dma((n, 2, nb + 1)),
            dma((n, n)), dma((nr, n)), dma((nc, nr, nb)), dma((n, nr, nb)), dma((nr,)), dma((2, nr)), dma((2, nr)),
            dma((nc, n)), dma((n, n)), dma((nr, n)), dma((nr, nc)), dma((nr, n)), dma, dma((2, 2)), dma,
        ],
        compiler_params=pltpu.CompilerParams(
            collective_id=0, has_side_effects=True, vmem_limit_bytes=VMEM_BYTES,
        ),
    )(a, b, row_gap, col_gap)


def local(amplitudes, integrals, tile_mask, occ_energy, virt_energy):
    nr = lax.axis_size("row")
    nc = lax.axis_size("col")
    r = lax.axis_index("row")
    c = lax.axis_index("col")
    depth, width = amplitudes.shape
    tile_rows = depth // TILE
    tile_cols = width // TILE
    own_mask = lax.dynamic_slice_in_dim(tile_mask, c * tile_rows, tile_rows, 0)
    keep_tiles = own_mask.astype(jnp.bfloat16)
    keep = jnp.broadcast_to(keep_tiles[:, :, None], (tile_rows, tile_cols, TILE)).reshape(tile_rows, 1, width)
    masked = (amplitudes.reshape(tile_rows, TILE, width) * keep).reshape(depth, width)
    q = width // nc
    pair_gap = (virt_energy[None, :] - occ_energy[:, None]).reshape(-1)
    col_gap = lax.dynamic_slice_in_dim(pair_gap, r * width, width, 0)[None, :]
    row_gap = jnp.stack([lax.dynamic_slice_in_dim(pair_gap, (r ^ m) * width + c * q, q, 0) for m in range(nr)])
    return fused(nr, nc, masked, integrals, row_gap[:, :, None], col_gap)[0]


def solution(mesh):
    return jax.shard_map(
        local,
        mesh=mesh,
        in_specs=(P("col", "row"), P("row", "col"), P(None, "row"), P(), P()),
        out_specs=P(("row", "col"), None),
        check_vma=False,
    )
```

```python
import functools

import jax
import jax.numpy as jnp
from jax import lax
from jax.experimental import pallas as pl
from jax.experimental.pallas import tpu as pltpu
from jax.sharding import PartitionSpec as P

TILE = 64
MESH = pl.DeviceIdType.MESH
VMEM_BYTES = 66_000_000
DIMS = (((0,), (0,)), ((), ()))


def xor(u, v, n):
    total, bit = 0, 1
    while bit < n:
        total = total + (((u // bit) % 2 + (v // bit) % 2) % 2) * bit
        bit *= 2
    return total


def bits_of(n):
    out, bit = [], 1
    while bit < n:
        out.append(bit)
        bit *= 2
    return out


def children(m, parity, n):
    if m == 0:
        return bits_of(n)
    have = [b for b in bits_of(n) if m & b]
    if parity == 0:
        return [b for b in bits_of(n) if b < have[0]]
    return [b for b in bits_of(n) if b > have[-1]]


def after(k, n):
    odd = k % 2 == 1
    up = jnp.where(k + 2 <= n - 1, k + 2, n - 2)
    down = jnp.where(k == 0, 1, k - 2)
    return jnp.where(odd, up, down)


def before(k, n):
    odd = k % 2 == 1
    up = jnp.where(k + 2 <= n - 2, k + 2, n - 1)
    down = jnp.where(k == 1, 0, k - 2)
    return jnp.where(odd, down, up)


def kernel(
    nr, nc, a_ref, b_ref, rg_ref, cg_ref, out, a_full, ib,
    ra, rb, ca, cb, stage, twin,
    s_tr, s_own, s_fwd, s_part, s_ra, s_rb, s_bc, s_hand, s_rra, s_rrb, s_po, s_out, s_tw,
    q_tr, q_a, q_g, q_q, q_ra, q_rb, q_out, l_c, l_r,
):
    r = lax.axis_index("row")
    c = lax.axis_index("col")
    n = nc // 2
    k = c // 2
    p = c % 2
    partner = c + 1 - 2 * p
    d, w = a_ref.shape
    e = b_ref.shape[0]
    eh = e // 2
    sub = w // n
    q = sub // 2
    half = n // 2
    depth = d * nc
    nxt, prv = before(k, n), after(k, n)
    low = k < half
    top_skip, bottom_skip = n - 2, 1
    mirrored = jnp.where(low, k, n - 1 - k)
    first = jnp.where(mirrored == 0, -1, 0)
    early = jnp.where(mirrored == 0, -1, n - 2 - mirrored)
    late = jnp.where(mirrored == 0, 0, mirrored + 1)
    bits = bits_of(nr)

    barrier = pltpu.get_barrier_semaphore()

    def greet(row, col):
        pl.semaphore_signal(barrier, inc=1, device_id=(row, col), device_id_type=MESH)

    greet(r, partner)
    for m in range(1, nr):
        greet(xor(r, m, nr), c)
        greet(xor(r, m, nr), partner)
    greet(r, (c + 2) % nc)
    greet(r, (c - 2 + nc) % nc)
    for t in range(2):
        greet(r, 2 * nxt + t)
        greet(r, 2 * prv + t)
    pl.semaphore_wait(barrier, 1 + 2 * (nr - 1) + 2 + 4)

    state = {"wait": False}

    def run(cond, body):
        if cond is None:
            body()
        else:
            pl.when(cond)(body)

    def both(*conds):
        total = None
        for x in conds:
            if x is None:
                continue
            total = x if total is None else jnp.logical_and(total, x)
        return total

    def no(x):
        return jnp.logical_not(x)

    def send(src, dst, sem, recv, row, col, cond=None):
        copy = pltpu.make_async_remote_copy(
            src_ref=src, dst_ref=dst, send_sem=sem, recv_sem=recv,
            device_id=(row, col), device_id_type=MESH,
        )
        run(cond, copy.wait_send if state["wait"] else copy.start)

    def local(src, dst, sem, cond=None):
        if not state["wait"]:
            run(cond, pltpu.make_async_copy(src, dst, sem).start)

    def arrived(ref, sem, cond=None):
        if not state["wait"]:
            run(cond, pltpu.make_async_copy(ref, ref, sem).wait)

    def ds(start, size):
        return pl.ds(pl.multiple_of(start, size), size)

    def a_rows(col):
        return ds(col * d, d)

    def b_rows(row):
        return ds(row * e, e)

    def cols(kp):
        return ds(kp * sub, sub)

    def h_rows(row, pp):
        return ds((2 * row + pp) * eh, eh)

    def raw(kk, kp, plane):
        direct = jnp.logical_and(kk == r, kp != plane)
        return ds(jnp.where(direct, 2 * r + p, 2 * nr + kk) * eh, eh)

    own = ds(c * q, q)

    def rows_a(src, col, cond):
        for x, b in enumerate(bits):
            send(src, ra.at[b, a_rows(col), :], s_ra.at[col, x], q_ra.at[b, col], xor(r, b, nr), c, cond)

    def b_out(src, kk, kp, cond):
        is_row = both(cond, kp == k)
        for t in range(2):
            part = src.at[:, pl.ds(t * q, q)]
            for x, b in enumerate(bits):
                row = xor(r, b, nr)
                send(
                    part, rb.at[xor(row, kk, nr), h_rows(r, p), :], s_rb.at[kk, t, x], q_rb.at[b, kk, p],
                    row, 2 * k + t, is_row,
                )
            dst = rb.at[xor(r, kk, nr), h_rows(r, p), :]
            local(part, dst, q_rb.at[0, kk, p], both(is_row, p == t))
            send(part, dst, s_rb.at[kk, t, len(bits)], q_rb.at[0, kk, p], r, partner, both(is_row, p != t))

    def spread(src, kk, kp, cond):
        ok = both(cond, kp != k, kp != prv)
        dst = ib.at[h_rows(r, p), cols(kp)]
        send(src, dst, s_bc.at[kk, kp], q_q.at[r, kp, p], kk, c, both(ok, kk != r))
        send(src, dst, s_bc.at[kk, kp], q_q.at[r, kp, p], r, partner, both(ok, kk == r))

    def mine_of(kp):
        return (
            (b_ref.at[ds(p * eh, eh), cols(kp % half)], owner(kp)),
            (ib.at[ds((2 * nr + k) * eh, eh), cols(kp)], no(owner(kp))),
        )

    def trade():
        other = 1 - p
        dst = ib.at[ds((2 * nr + k) * eh, eh), ds(p * (w // 2), w // 2)]
        send(b_ref.at[ds(other * eh, eh), :], dst, s_tr, q_tr, r, partner)
        arrived(dst, q_tr)

    def blocked(target, kp):
        return jnp.logical_or(
            jnp.logical_and(target == 0, kp == bottom_skip),
            jnp.logical_and(target == n - 1, kp == top_skip),
        )

    def owner(kp):
        return kp // half == p

    def piece(sign, j):
        return n - 1 - j if sign > 0 else j

    def swap(j):
        return jnp.where(j == 1, 2, jnp.where(j == 2, 1, j))

    def edge(sign):
        return 0 if sign > 0 else n - 1

    def valid(j):
        return jnp.logical_and(j >= 0, j < n)

    def clip(x, top):
        return jnp.clip(x, 0, top)

    def issue_own(sign, j, when=None):
        ok = both(valid(j), when)
        kp = piece(sign, jnp.where(k == edge(sign), swap(clip(j, n - 1)), clip(j, n - 1)))
        far = k + sign
        ok = both(ok, far >= 0, far < n, no(blocked(far, kp)))
        x = 0 if sign > 0 else 1
        target = clip(c + 2 * sign, nc - 1)
        send(a_ref.at[:, cols(kp)], a_full.at[a_rows(c), cols(kp)], s_own.at[x, 0, kp], q_a.at[c, kp], r, target, ok)
        for src, cond in mine_of(kp):
            send(
                src, ib.at[raw(k, kp, far), cols(kp)], s_own.at[x, 1, kp], q_g.at[k, kp],
                r, target, both(ok, cond),
            )

    def order(sign, j, s, src):
        j = clip(j, n - 1)
        return piece(sign, jnp.where(src == edge(sign), swap(j), j) if s == 1 else j)

    def relay(sign, j, s, tau):
        src = k - sign * s
        kp = order(sign, j, s, src)
        here = both(valid(j), src >= 0, src < n, no(blocked(k, kp)))
        kk = clip(src, n - 1)
        far = k + sign
        x = 0 if sign > 0 else 1
        target = clip(c + 2 * sign, nc - 1)
        col = 2 * kk + p

        def onward(which, kp, cond):
            ok = both(cond, valid(j), src >= 0, src < n, far >= 0, far < n, no(blocked(far, kp)))
            if which == 0:
                ref = a_full.at[a_rows(col), cols(kp)]
                send(ref, ref, s_fwd.at[x, s - 1, 0, kp], q_a.at[col, kp], r, target, ok)
            else:
                send(
                    ib.at[raw(kk, kp, k), cols(kp)], ib.at[raw(kk, kp, far), cols(kp)],
                    s_fwd.at[x, s - 1, 1, kp], q_g.at[kk, kp], r, target, ok,
                )

        held = both(src == edge(sign), j == 1) if s == 1 else None
        freed = both(src == edge(sign), j == 2)
        a_piece = a_full.at[a_rows(col), cols(kp)]
        arrived(a_piece, q_a.at[col, kp], here)
        onward(0, kp, no(held) if s == 1 else None)
        send(a_piece, a_piece, s_part.at[kk, kp], q_a.at[col, kp], r, partner, both(here, kp != prv))
        rows_a(a_full.at[a_rows(col), own], col, both(here, kp == k))
        b_piece = ib.at[raw(kk, kp, k), cols(kp)]
        arrived(b_piece, q_g.at[kk, kp], here)
        onward(1, kp, no(held) if s == 1 else None)
        if s == 1:
            onward(0, order(sign, 1, 1, src), freed)
            onward(1, order(sign, 1, 1, src), freed)
        issue_own(sign, j + 1, both(valid(j), src == edge(sign)))
        b_out(b_piece, kk, kp, here)
        spread(b_piece, kk, kp, both(here, tau > late))

    def partner_rows(kk, cond):
        col = 2 * kk + 1 - p
        ref = a_full.at[a_rows(col), cols(k)]
        arrived(ref, q_a.at[col, k], cond)
        rows_a(a_full.at[a_rows(col), own], col, cond)

    def own_part():
        rows_a(a_ref.at[:, own], c, None)

        @pl.loop(0, n)
        def _(kp):
            for src, cond in mine_of(kp):
                b_out(src, k, kp, cond)
                local(src, ib.at[h_rows(r, p), cols(kp)], q_q.at[r, kp, p], both(cond, k == r, kp != k, kp != prv))
            part = a_ref.at[:, cols(kp)]
            dst = a_full.at[a_rows(c), cols(kp)]
            send(part, dst, s_part.at[k, kp], q_a.at[c, kp], r, partner, kp != prv)
            local(part, dst, q_a.at[c, kp], kp != prv)

    def slot(tau):
        up = tau + jnp.where(low, 1, 0)
        down = tau + jnp.where(low, 0, 1)
        issue_own(1, up + 1, both(valid(up), k == 0))
        issue_own(-1, down + 1, both(valid(down), k == n - 1))
        for s in range(1, n):
            relay(1, up, s, tau)
            relay(-1, down, s, tau)
        for s in range(1, n):
            for sign, j in ((1, up), (-1, down)):
                src = k - sign * s
                cond = both(valid(j), src >= 0, src < n, order(sign, j, s, src) == k)
                partner_rows(clip(src, n - 1), cond)

    def pass_rows(kk, m, cond):
        origin = xor(r, m, nr)
        for pp in range(2):
            if m:
                col = 2 * kk + pp
                got = ra.at[m, a_rows(col), :]
                arrived(got, q_ra.at[m, col], cond)
                for b in children(m, pp, nr):
                    x = bits.index(b)
                    send(
                        got, ra.at[m | b, a_rows(col), :], s_rra.at[col, m, x], q_ra.at[m | b, col],
                        xor(r, b, nr), c, cond,
                    )
            got = rb.at[xor(r, kk, nr), h_rows(origin, pp), :]
            arrived(got, q_rb.at[m, kk, pp], cond)
            if m:
                for b in children(m, pp, nr):
                    x = bits.index(b)
                    row = xor(r, b, nr)
                    send(
                        got, rb.at[xor(row, kk, nr), h_rows(origin, pp), :], s_rrb.at[kk, m, pp, x],
                        q_rb.at[m | b, kk, pp], row, c, cond,
                    )
            dst = ib.at[h_rows(origin, pp), own]
            send(got, dst, s_po.at[m, pp], q_q.at[origin, k, pp], r, partner, both(cond, kk == r))

    def pass_direct(tau):
        @pl.loop(0, n)
        def _(kk):
            near = jnp.where((kk < k) == low, early, late)
            when = jnp.where(kk == k, first, near)
            for m in bits:
                pass_rows(kk, m, tau == when)

    def pass_rest():
        @pl.loop(0, n)
        def _(kk):
            for m in range(nr):
                if m not in bits:
                    pass_rows(kk, m, None)

    def spread_all(tau):
        @pl.loop(0, n)
        def _(kp):
            for m in [*range(1, nr), 0]:
                kk = xor(r, m, nr)
                up = jnp.where(jnp.logical_and(kk == 0, k == 1), swap(n - 1 - kp), n - 1 - kp)
                down = jnp.where(jnp.logical_and(kk == n - 1, k == n - 2), swap(kp), kp)
                came = jnp.where(kk < k, up - jnp.where(low, 1, 0), down - jnp.where(low, 0, 1))
                ok = both(tau == late, no(blocked(k, kp)))
                for src, cond in mine_of(kp):
                    spread(src, kk, kp, both(ok, kk == k, cond))
                there = ib.at[raw(kk, kp, k), cols(kp)]
                spread(there, kk, kp, both(ok, kk != k, came <= late))

    def hand(kp, cond):
        for m in range(nr):
            row = xor(r, m, nr)
            ref = ib.at[h_rows(row, p), cols(kp)]
            if m:
                arrived(ref, q_q.at[row, kp, p], cond)
                send(ref, ref, s_hand.at[row, kp], q_q.at[row, kp, p], r, partner, cond)
            else:
                arrived(ref, q_q.at[row, kp, p], both(cond, k == r))

    def tile_piece(t):
        rank = jnp.where(low, prv, n - 1 - prv)
        base = jnp.where(mirrored < rank, mirrored, mirrored - 1)
        i = jnp.where(t == 0, base, jnp.where(t <= base, t - 1, t))
        i = jnp.where(i >= rank, i + 1, i)
        return jnp.where(low, i, n - 1 - i)

    def tile(t):
        kp = tile_piece(t)
        is_own = kp == k
        for kk in range(n):
            col = 2 * kk + 1 - p
            arrived(a_full.at[a_rows(col), cols(kp)], q_a.at[col, kp], no(is_own))
        arrived(a_full.at[a_rows(c), cols(kp)], q_a.at[c, kp], no(is_own))
        for row in range(nr):
            arrived(ib.at[h_rows(row, 1 - p), cols(kp)], q_q.at[row, kp, 1 - p], no(is_own))
            for pp in range(2):
                arrived(ib.at[h_rows(row, pp), own], q_q.at[row, k, pp], is_own)

        def load(h):
            where = ds((2 * kp + h) * q, q)
            full = pl.ds(0, depth)
            pltpu.make_async_copy(a_full.at[:, where], ca.at[h], l_c.at[h, 0]).start()
            mine = jnp.logical_and(is_own, p == h)
            run(mine, pltpu.make_async_copy(rb.at[0], cb.at[h], l_c.at[h, 1]).start)
            run(no(mine), pltpu.make_async_copy(ib.at[full, where], cb.at[h], l_c.at[h, 1]).start)

        for h in range(2):
            load(h)

        @pl.loop(0, 2)
        def _(h):
            where = ds((2 * kp + h) * q, q)
            pltpu.make_async_copy(ca.at[h], ca.at[h], l_c.at[h, 0]).wait()
            pltpu.make_async_copy(cb.at[h], cb.at[h], l_c.at[h, 1]).wait()

            @pl.loop(0, nr)
            def _(i):
                m = nr - 1 - i
                row = xor(r, m, nr)
                buf = stage.at[h, m]
                run(t > 0, pltpu.make_async_copy(buf, buf, s_out.at[h, m]).wait)
                total = lax.dot_general(ra[m], cb[h], DIMS, preferred_element_type=jnp.float32)
                total += lax.dot_general(rb[m], ca[h], DIMS, preferred_element_type=jnp.float32)
                total = total / (rg_ref[m] + cg_ref[:, where])
                stage[h, m] = total.astype(stage.dtype)
                dst = out.at[:, ds(r * w + (2 * kp + h) * q, q)]
                remote = pltpu.make_async_remote_copy(
                    src_ref=buf, dst_ref=dst, send_sem=s_out.at[h, m], recv_sem=q_out,
                    device_id=(row, c), device_id_type=MESH,
                )
                run(m > 0, remote.start)
                run(m == 0, pltpu.make_async_copy(buf, dst, s_out.at[h, m]).start)

                @pl.when(kp == nxt)
                def _():
                    twin[h, m] = total.T.astype(twin.dtype)
                    pltpu.make_async_remote_copy(
                        src_ref=twin.at[h, m], dst_ref=out.at[:, ds(row * w + c * q, q)],
                        send_sem=s_tw.at[h, m], recv_sem=q_out,
                        device_id=(r, 2 * kp + h), device_id_type=MESH,
                    ).start()

    end = mirrored == 0

    def start():
        trade()
        for sign in (1, -1):
            issue_own(sign, jnp.int32(0))
        own_part()
        partner_rows(k, None)

    start()

    @pl.loop(0, jnp.where(end, n + 1, n + 2))
    def _(x):
        slot(x - 2)
        pass_direct(x - 2)
        spread_all(x - 2)

    pass_rest()
    arrived(a_full.at[a_rows(c), cols(k)], q_a.at[c, k])
    load_own = pltpu.make_async_copy(a_full.at[:, own], ra.at[0], l_r)
    load_own.start()
    load_own.wait()

    @pl.loop(0, jnp.where(end, n, n - 1))
    def _(x):
        last = jnp.logical_and(end, x == 2)

        @pl.when(last)
        def _():
            slot(x * 0 + n - 1)

        @pl.when(no(last))
        def _():
            t = jnp.where(jnp.logical_and(end, x > 2), x - 1, x)
            hand(tile_piece(t), t > 0)
            tile(t)

    state["wait"] = True
    start()

    @pl.loop(0, n + 2)
    def _(x):
        slot(x - 2)
        pass_direct(x - 2)
        spread_all(x - 2)

    pass_rest()

    @pl.loop(1, n - 1)
    def _(t):
        hand(tile_piece(t), None)

    @pl.loop(0, 2)
    def _(h):
        @pl.loop(0, nr)
        def _(m):
            pltpu.make_async_copy(stage.at[h, m], stage.at[h, m], s_out.at[h, m]).wait()
            pltpu.make_async_copy(twin.at[h, m], twin.at[h, m], s_tw.at[h, m]).wait()

    landed = out.at[:, pl.ds(0, (nr - 1) * (n - 1) * sub + nr * sub)]
    pltpu.make_async_copy(landed, landed, q_out).wait()


def fused(nr, nc, a, b, row_gap, col_gap):
    d, w = a.shape
    e = b.shape[0]
    n = nc // 2
    depth = d * nc
    q = w // nc
    nb = len(bits_of(nr))
    dma = pltpu.SemaphoreType.DMA
    hbm = pl.BlockSpec(memory_space=pl.ANY)
    vmem = pl.BlockSpec(memory_space=pltpu.VMEM)
    shapes = [(q, nr * w), (depth, w), (nr * e + n * e // 2, w)]
    block = pltpu.VMEM((nr, depth, q), a.dtype)
    pair = pltpu.VMEM((2, depth, q), a.dtype)
    tiles = pltpu.VMEM((2, nr, q, q), a.dtype)
    return pl.pallas_call(
        functools.partial(kernel, nr, nc),
        out_shape=[jax.ShapeDtypeStruct(s, a.dtype) for s in shapes],
        in_specs=[hbm, hbm, vmem, vmem],
        out_specs=[hbm] * 3,
        scratch_shapes=[
            block, block, pair, pair, tiles, tiles,
            dma, dma((2, 2, n)), dma((2, n - 1, 2, n)), dma((n, n)), dma((nc, nb)), dma((n, 2, nb + 1)),
            dma((n, n)), dma((nr, n)), dma((nc, nr, nb)), dma((n, nr, 2, nb)), dma((nr, 2)), dma((2, nr)), dma((2, nr)),
            dma, dma((nc, n)), dma((n, n)), dma((nr, n, 2)), dma((nr, nc)), dma((nr, n, 2)), dma, dma((2, 2)), dma,
        ],
        compiler_params=pltpu.CompilerParams(
            collective_id=0, has_side_effects=True, vmem_limit_bytes=VMEM_BYTES,
        ),
    )(a, b, row_gap, col_gap)


def local(amplitudes, integrals, tile_mask, occ_energy, virt_energy):
    nr = lax.axis_size("row")
    nc = lax.axis_size("col")
    r = lax.axis_index("row")
    c = lax.axis_index("col")
    depth, width = amplitudes.shape
    tile_rows = depth // TILE
    tile_cols = width // TILE
    own_mask = lax.dynamic_slice_in_dim(tile_mask, c * tile_rows, tile_rows, 0)
    keep_tiles = own_mask.astype(jnp.bfloat16)
    keep = jnp.broadcast_to(keep_tiles[:, :, None], (tile_rows, tile_cols, TILE)).reshape(tile_rows, 1, width)
    masked = (amplitudes.reshape(tile_rows, TILE, width) * keep).reshape(depth, width)
    q = width // nc
    pair_gap = (virt_energy[None, :] - occ_energy[:, None]).reshape(-1)
    col_gap = lax.dynamic_slice_in_dim(pair_gap, r * width, width, 0)[None, :]
    row_gap = jnp.stack([lax.dynamic_slice_in_dim(pair_gap, (r ^ m) * width + c * q, q, 0) for m in range(nr)])
    return fused(nr, nc, masked, integrals, row_gap[:, :, None], col_gap)[0]


def solution(mesh):
    return jax.shard_map(
        local,
        mesh=mesh,
        in_specs=(P("col", "row"), P("row", "col"), P(None, "row"), P(), P()),
        out_specs=P(("row", "col"), None),
        check_vma=False,
    )
```

```python
import functools

import jax
import jax.numpy as jnp
from jax import lax
from jax.experimental import pallas as pl
from jax.experimental.pallas import tpu as pltpu
from jax.sharding import PartitionSpec as P

TILE = 64
MESH = pl.DeviceIdType.MESH
VMEM_BYTES = 66_000_000
DIMS = (((0,), (0,)), ((), ()))


def xor(u, v, n):
    total, bit = 0, 1
    while bit < n:
        total = total + (((u // bit) % 2 + (v // bit) % 2) % 2) * bit
        bit *= 2
    return total


def bits_of(n):
    out, bit = [], 1
    while bit < n:
        out.append(bit)
        bit *= 2
    return out


def children(m, parity, n):
    if m == 0:
        return bits_of(n)
    have = [b for b in bits_of(n) if m & b]
    if parity == 0:
        return [b for b in bits_of(n) if b < have[0]]
    return [b for b in bits_of(n) if b > have[-1]]


def after(k, n):
    odd = k % 2 == 1
    up = jnp.where(k + 2 <= n - 1, k + 2, n - 2)
    down = jnp.where(k == 0, 1, k - 2)
    return jnp.where(odd, up, down)


def before(k, n):
    odd = k % 2 == 1
    up = jnp.where(k + 2 <= n - 2, k + 2, n - 1)
    down = jnp.where(k == 1, 0, k - 2)
    return jnp.where(odd, down, up)


def kernel(
    nr, nc, a_ref, b_ref, rg_ref, cg_ref, out, a_full, ib,
    ra, rb, ca, cb, stage, twin,
    s_tr, s_own, s_fwd, s_part, s_ra, s_rb, s_bc, s_hand, s_rra, s_rrb, s_po, s_out, s_tw,
    q_tr, q_a, q_g, q_q, q_ra, q_rb, q_out, l_c, l_r,
):
    r = lax.axis_index("row")
    c = lax.axis_index("col")
    n = nc // 2
    k = c // 2
    p = c % 2
    partner = c + 1 - 2 * p
    d, w = a_ref.shape
    e = b_ref.shape[0]
    eh = e // 2
    sub = w // n
    q = sub // 2
    half = n // 2
    depth = d * nc
    nxt, prv = before(k, n), after(k, n)
    low = k < half
    top_skip, bottom_skip = n - 2, 1
    mirrored = jnp.where(low, k, n - 1 - k)
    first = jnp.where(mirrored == 0, -1, 0)
    early = jnp.where(mirrored == 0, -1, n - 2 - mirrored)
    late = jnp.where(mirrored == 0, 0, mirrored + 1)
    bits = bits_of(nr)

    barrier = pltpu.get_barrier_semaphore()

    def greet(row, col):
        pl.semaphore_signal(barrier, inc=1, device_id=(row, col), device_id_type=MESH)

    greet(r, partner)
    for m in range(1, nr):
        greet(xor(r, m, nr), c)
        greet(xor(r, m, nr), partner)
    greet(r, (c + 2) % nc)
    greet(r, (c - 2 + nc) % nc)
    for t in range(2):
        greet(r, 2 * nxt + t)
        greet(r, 2 * prv + t)
    pl.semaphore_wait(barrier, 1 + 2 * (nr - 1) + 2 + 4)

    state = {"wait": False}

    def run(cond, body):
        if cond is None:
            body()
        else:
            pl.when(cond)(body)

    def both(*conds):
        total = None
        for x in conds:
            if x is None:
                continue
            total = x if total is None else jnp.logical_and(total, x)
        return total

    def no(x):
        return jnp.logical_not(x)

    def send(src, dst, sem, recv, row, col, cond=None):
        copy = pltpu.make_async_remote_copy(
            src_ref=src, dst_ref=dst, send_sem=sem, recv_sem=recv,
            device_id=(row, col), device_id_type=MESH,
        )
        run(cond, copy.wait_send if state["wait"] else copy.start)

    def local(src, dst, sem, cond=None):
        if not state["wait"]:
            run(cond, pltpu.make_async_copy(src, dst, sem).start)

    def arrived(ref, sem, cond=None):
        if not state["wait"]:
            run(cond, pltpu.make_async_copy(ref, ref, sem).wait)

    def ds(start, size):
        return pl.ds(pl.multiple_of(start, size), size)

    def a_rows(col):
        return ds(col * d, d)

    def b_rows(row):
        return ds(row * e, e)

    def cols(kp):
        return ds(kp * sub, sub)

    def h_rows(row, pp):
        return ds((2 * row + pp) * eh, eh)

    def raw(kk, kp, plane):
        direct = jnp.logical_and(kk == r, kp != plane)
        return ds(jnp.where(direct, 2 * r + p, 2 * nr + kk) * eh, eh)

    own = ds(c * q, q)

    def rows_a(src, col, cond):
        for x, b in enumerate(bits):
            send(src, ra.at[b, a_rows(col), :], s_ra.at[col, x], q_ra.at[b, col], xor(r, b, nr), c, cond)

    def b_out(src, kk, kp, cond):
        is_row = both(cond, kp == k)
        for t in range(2):
            part = src.at[:, pl.ds(t * q, q)]
            for x, b in enumerate(bits):
                row = xor(r, b, nr)
                send(
                    part, rb.at[xor(row, kk, nr), h_rows(r, p), :], s_rb.at[kk, t, x], q_rb.at[b, kk, p],
                    row, 2 * k + t, is_row,
                )
            dst = rb.at[xor(r, kk, nr), h_rows(r, p), :]
            local(part, dst, q_rb.at[0, kk, p], both(is_row, p == t))
            send(part, dst, s_rb.at[kk, t, len(bits)], q_rb.at[0, kk, p], r, partner, both(is_row, p != t))

    def spread(src, kk, kp, cond):
        ok = both(cond, kp != k, kp != prv)
        dst = ib.at[h_rows(r, p), cols(kp)]
        send(src, dst, s_bc.at[kk, kp], q_q.at[r, kp, p], kk, c, both(ok, kk != r))
        send(src, dst, s_bc.at[kk, kp], q_q.at[r, kp, p], r, partner, both(ok, kk == r))

    def mine_of(kp):
        return (
            (b_ref.at[ds(p * eh, eh), cols(kp % half)], owner(kp)),
            (ib.at[ds((2 * nr + k) * eh, eh), cols(kp)], no(owner(kp))),
        )

    def trade():
        other = 1 - p
        dst = ib.at[ds((2 * nr + k) * eh, eh), ds(p * (w // 2), w // 2)]
        send(b_ref.at[ds(other * eh, eh), :], dst, s_tr, q_tr, r, partner)
        arrived(dst, q_tr)

    def blocked(target, kp):
        return jnp.logical_or(
            jnp.logical_and(target == 0, kp == bottom_skip),
            jnp.logical_and(target == n - 1, kp == top_skip),
        )

    def owner(kp):
        return kp // half == p

    def piece(sign, j):
        return jnp.where(sign > 0, n - 1 - j, j)

    def swap(j):
        return jnp.where(j == 1, 2, jnp.where(j == 2, 1, j))

    def edge(sign):
        return jnp.where(sign > 0, 0, n - 1)

    def valid(j):
        return jnp.logical_and(j >= 0, j < n)

    def clip(x, top):
        return jnp.clip(x, 0, top)

    def issue_own(sign, j, when=None):
        ok = both(valid(j), when)
        kp = piece(sign, jnp.where(k == edge(sign), swap(clip(j, n - 1)), clip(j, n - 1)))
        far = k + sign
        ok = both(ok, far >= 0, far < n, no(blocked(far, kp)))
        x = jnp.where(sign > 0, 0, 1)
        target = clip(c + 2 * sign, nc - 1)
        send(a_ref.at[:, cols(kp)], a_full.at[a_rows(c), cols(kp)], s_own.at[x, 0, kp], q_a.at[c, kp], r, target, ok)
        for src, cond in mine_of(kp):
            send(
                src, ib.at[raw(k, kp, far), cols(kp)], s_own.at[x, 1, kp], q_g.at[k, kp],
                r, target, both(ok, cond),
            )

    def order(sign, j, s, src):
        j = clip(j, n - 1)
        return piece(sign, jnp.where(src == edge(sign), swap(j), j) if s == 1 else j)

    def relay(sign, j, s, tau, go):
        src = jnp.where(go, k - sign * s, -1)
        kp = order(sign, j, s, src)
        here = both(valid(j), src >= 0, src < n, no(blocked(k, kp)))
        kk = clip(src, n - 1)
        far = k + sign
        x = jnp.where(sign > 0, 0, 1)
        target = clip(c + 2 * sign, nc - 1)
        col = 2 * kk + p

        def onward(which, kp, cond):
            ok = both(cond, valid(j), src >= 0, src < n, far >= 0, far < n, no(blocked(far, kp)))
            if which == 0:
                ref = a_full.at[a_rows(col), cols(kp)]
                send(ref, ref, s_fwd.at[x, s - 1, 0, kp], q_a.at[col, kp], r, target, ok)
            else:
                send(
                    ib.at[raw(kk, kp, k), cols(kp)], ib.at[raw(kk, kp, far), cols(kp)],
                    s_fwd.at[x, s - 1, 1, kp], q_g.at[kk, kp], r, target, ok,
                )

        held = both(src == edge(sign), j == 1) if s == 1 else None
        freed = both(src == edge(sign), j == 2)
        a_piece = a_full.at[a_rows(col), cols(kp)]
        arrived(a_piece, q_a.at[col, kp], here)
        onward(0, kp, no(held) if s == 1 else None)
        send(a_piece, a_piece, s_part.at[kk, kp], q_a.at[col, kp], r, partner, both(here, kp != prv))
        rows_a(a_full.at[a_rows(col), own], col, both(here, kp == k))
        b_piece = ib.at[raw(kk, kp, k), cols(kp)]
        arrived(b_piece, q_g.at[kk, kp], here)
        onward(1, kp, no(held) if s == 1 else None)
        last = both(valid(j), src == edge(sign))
        if s == 1:
            issue_own(sign, 2, freed)
            onward(0, order(sign, 1, 1, src), freed)
            onward(1, order(sign, 1, 1, src), freed)
            issue_own(sign, j + 1, both(last, j != 1))
        else:
            issue_own(sign, j + jnp.where(far == edge(-sign), 2, 1), last)
        b_out(b_piece, kk, kp, here)
        spread(b_piece, kk, kp, both(here, tau > late))

    def partner_rows(kk, cond):
        col = 2 * kk + 1 - p
        ref = a_full.at[a_rows(col), cols(k)]
        arrived(ref, q_a.at[col, k], cond)
        rows_a(a_full.at[a_rows(col), own], col, cond)

    def own_part():
        rows_a(a_ref.at[:, own], c, None)

        @pl.loop(0, n)
        def _(kp):
            for src, cond in mine_of(kp):
                b_out(src, k, kp, cond)
                local(src, ib.at[h_rows(r, p), cols(kp)], q_q.at[r, kp, p], both(cond, k == r, kp != k, kp != prv))
            part = a_ref.at[:, cols(kp)]
            dst = a_full.at[a_rows(c), cols(kp)]
            send(part, dst, s_part.at[k, kp], q_a.at[c, kp], r, partner, kp != prv)
            local(part, dst, q_a.at[c, kp], kp != prv)

    def slot(tau, lo=1, hi=None):
        lag = jnp.where(low, -1, 1)
        ways = ((lag, tau), (-lag, tau + 1))
        hi = n - 1 if hi is None else hi
        for s in range(1, n):
            go = jnp.logical_and(s >= lo, s <= hi)
            for sign, j in ways:
                relay(sign, j, s, tau, go)
        for s in range(1, n):
            go = jnp.logical_and(s >= lo, s <= hi)
            for sign, j in ways:
                src = jnp.where(go, k - sign * s, -1)
                cond = both(valid(j), src >= 0, src < n, order(sign, j, s, src) == k)
                partner_rows(clip(src, n - 1), cond)

    def pass_rows(kk, m, cond):
        origin = xor(r, m, nr)
        for pp in range(2):
            if m:
                col = 2 * kk + pp
                got = ra.at[m, a_rows(col), :]
                arrived(got, q_ra.at[m, col], cond)
                for b in children(m, pp, nr):
                    x = bits.index(b)
                    send(
                        got, ra.at[m | b, a_rows(col), :], s_rra.at[col, m, x], q_ra.at[m | b, col],
                        xor(r, b, nr), c, cond,
                    )
            got = rb.at[xor(r, kk, nr), h_rows(origin, pp), :]
            arrived(got, q_rb.at[m, kk, pp], cond)
            if m:
                for b in children(m, pp, nr):
                    x = bits.index(b)
                    row = xor(r, b, nr)
                    send(
                        got, rb.at[xor(row, kk, nr), h_rows(origin, pp), :], s_rrb.at[kk, m, pp, x],
                        q_rb.at[m | b, kk, pp], row, c, cond,
                    )
            dst = ib.at[h_rows(origin, pp), own]
            send(got, dst, s_po.at[m, pp], q_q.at[origin, k, pp], r, partner, both(cond, kk == r))

    def pass_direct(tau):
        @pl.loop(0, n)
        def _(kk):
            near = jnp.where((kk < k) == low, early, late)
            when = jnp.where(kk == k, first, near)
            for m in bits:
                pass_rows(kk, m, tau == when)

    def pass_rest():
        @pl.loop(0, n)
        def _(kk):
            for m in range(nr):
                if m not in bits:
                    pass_rows(kk, m, None)

    def spread_all(tau):
        @pl.loop(0, n)
        def _(kp):
            for m in [*range(1, nr), 0]:
                kk = xor(r, m, nr)
                up = jnp.where(jnp.logical_and(kk == 0, k == 1), swap(n - 1 - kp), n - 1 - kp)
                down = jnp.where(jnp.logical_and(kk == n - 1, k == n - 2), swap(kp), kp)
                came = jnp.where(kk < k, up - jnp.where(low, 1, 0), down - jnp.where(low, 0, 1))
                ok = both(tau == late, no(blocked(k, kp)))
                for src, cond in mine_of(kp):
                    spread(src, kk, kp, both(ok, kk == k, cond))
                there = ib.at[raw(kk, kp, k), cols(kp)]
                spread(there, kk, kp, both(ok, kk != k, came <= late))

    def hand(kp, cond):
        for m in range(nr):
            row = xor(r, m, nr)
            ref = ib.at[h_rows(row, p), cols(kp)]
            if m:
                arrived(ref, q_q.at[row, kp, p], cond)
                send(ref, ref, s_hand.at[row, kp], q_q.at[row, kp, p], r, partner, cond)
            else:
                arrived(ref, q_q.at[row, kp, p], both(cond, k == r))

    def tile_piece(t):
        rank = jnp.where(low, prv, n - 1 - prv)
        base = jnp.where(mirrored < rank, mirrored, mirrored - 1)
        i = jnp.where(t == 0, base, jnp.where(t <= base, t - 1, t))
        i = jnp.where(i >= rank, i + 1, i)
        return jnp.where(low, i, n - 1 - i)

    def tile(t):
        kp = tile_piece(t)
        is_own = kp == k
        for kk in range(n):
            col = 2 * kk + 1 - p
            arrived(a_full.at[a_rows(col), cols(kp)], q_a.at[col, kp], no(is_own))
        arrived(a_full.at[a_rows(c), cols(kp)], q_a.at[c, kp], no(is_own))
        for row in range(nr):
            arrived(ib.at[h_rows(row, 1 - p), cols(kp)], q_q.at[row, kp, 1 - p], no(is_own))
            for pp in range(2):
                arrived(ib.at[h_rows(row, pp), own], q_q.at[row, k, pp], is_own)

        def load(h):
            where = ds((2 * kp + h) * q, q)
            full = pl.ds(0, depth)
            pltpu.make_async_copy(a_full.at[:, where], ca.at[h], l_c.at[h, 0]).start()
            mine = jnp.logical_and(is_own, p == h)
            run(mine, pltpu.make_async_copy(rb.at[0], cb.at[h], l_c.at[h, 1]).start)
            run(no(mine), pltpu.make_async_copy(ib.at[full, where], cb.at[h], l_c.at[h, 1]).start)

        for h in range(2):
            load(h)

        @pl.loop(0, 2)
        def _(h):
            where = ds((2 * kp + h) * q, q)
            pltpu.make_async_copy(ca.at[h], ca.at[h], l_c.at[h, 0]).wait()
            pltpu.make_async_copy(cb.at[h], cb.at[h], l_c.at[h, 1]).wait()

            @pl.loop(0, nr)
            def _(i):
                m = nr - 1 - i
                row = xor(r, m, nr)
                buf = stage.at[h, m]
                run(t > 0, pltpu.make_async_copy(buf, buf, s_out.at[h, m]).wait)
                total = lax.dot_general(ra[m], cb[h], DIMS, preferred_element_type=jnp.float32)
                total += lax.dot_general(rb[m], ca[h], DIMS, preferred_element_type=jnp.float32)
                total = total / (rg_ref[m] + cg_ref[:, where])
                stage[h, m] = total.astype(stage.dtype)
                dst = out.at[:, ds(r * w + (2 * kp + h) * q, q)]
                remote = pltpu.make_async_remote_copy(
                    src_ref=buf, dst_ref=dst, send_sem=s_out.at[h, m], recv_sem=q_out,
                    device_id=(row, c), device_id_type=MESH,
                )
                run(m > 0, remote.start)
                run(m == 0, pltpu.make_async_copy(buf, dst, s_out.at[h, m]).start)

                @pl.when(kp == nxt)
                def _():
                    twin[h, m] = total.T.astype(twin.dtype)
                    pltpu.make_async_remote_copy(
                        src_ref=twin.at[h, m], dst_ref=out.at[:, ds(row * w + c * q, q)],
                        send_sem=s_tw.at[h, m], recv_sem=q_out,
                        device_id=(r, 2 * kp + h), device_id_type=MESH,
                    ).start()

    end = mirrored == 0

    def start():
        trade()
        for sign in (1, -1):
            for j in range(n):
                issue_own(jnp.int32(sign), jnp.int32(j), None if j == 0 else k == edge(sign))
        own_part()
        partner_rows(k, None)

    start()

    @pl.loop(0, n + 2)
    def _(x):
        i = x - 3
        ahead = jnp.logical_and(end, i >= 0)
        final = i == n - 2
        tau = jnp.where(ahead, jnp.where(final, 2, i + 2), x - 2)
        lo = jnp.where(jnp.logical_and(ahead, final), 2, 1)
        hi = jnp.where(jnp.logical_and(final, no(end)), 1, jnp.where(jnp.logical_and(ahead, no(final)), 1, n - 1))
        slot(tau, lo, hi)
        fresh = jnp.where(ahead, n, tau)
        pass_direct(fresh)
        spread_all(fresh)

    pass_rest()
    arrived(a_full.at[a_rows(c), cols(k)], q_a.at[c, k])
    load_own = pltpu.make_async_copy(a_full.at[:, own], ra.at[0], l_r)
    load_own.start()
    load_own.wait()

    @pl.loop(0, jnp.where(end, n, n - 1))
    def _(x):
        @pl.when(jnp.logical_or(jnp.logical_and(end, jnp.logical_and(x > 1, x < n - 1)), jnp.logical_and(no(end), x == 1)))
        def _():
            slot(jnp.where(end, x + 1, n - 1), 2)

        @pl.when(no(jnp.logical_and(end, x == 1)))
        def _():
            t = jnp.where(jnp.logical_and(end, x > 1), x - 1, x)
            hand(tile_piece(t), t > 0)
            tile(t)

    state["wait"] = True
    start()

    @pl.loop(0, n + 2)
    def _(x):
        slot(x - 2)
        pass_direct(x - 2)
        spread_all(x - 2)

    pass_rest()

    @pl.loop(1, n - 1)
    def _(t):
        hand(tile_piece(t), None)

    @pl.loop(0, 2)
    def _(h):
        @pl.loop(0, nr)
        def _(m):
            pltpu.make_async_copy(stage.at[h, m], stage.at[h, m], s_out.at[h, m]).wait()
            pltpu.make_async_copy(twin.at[h, m], twin.at[h, m], s_tw.at[h, m]).wait()

    landed = out.at[:, pl.ds(0, (nr - 1) * (n - 1) * sub + nr * sub)]
    pltpu.make_async_copy(landed, landed, q_out).wait()


def fused(nr, nc, a, b, row_gap, col_gap):
    d, w = a.shape
    e = b.shape[0]
    n = nc // 2
    depth = d * nc
    q = w // nc
    nb = len(bits_of(nr))
    dma = pltpu.SemaphoreType.DMA
    hbm = pl.BlockSpec(memory_space=pl.ANY)
    vmem = pl.BlockSpec(memory_space=pltpu.VMEM)
    shapes = [(q, nr * w), (depth, w), (nr * e + n * e // 2, w)]
    block = pltpu.VMEM((nr, depth, q), a.dtype)
    pair = pltpu.VMEM((2, depth, q), a.dtype)
    tiles = pltpu.VMEM((2, nr, q, q), a.dtype)
    return pl.pallas_call(
        functools.partial(kernel, nr, nc),
        out_shape=[jax.ShapeDtypeStruct(s, a.dtype) for s in shapes],
        in_specs=[hbm, hbm, vmem, vmem],
        out_specs=[hbm] * 3,
        scratch_shapes=[
            block, block, pair, pair, tiles, tiles,
            dma, dma((2, 2, n)), dma((2, n - 1, 2, n)), dma((n, n)), dma((nc, nb)), dma((n, 2, nb + 1)),
            dma((n, n)), dma((nr, n)), dma((nc, nr, nb)), dma((n, nr, 2, nb)), dma((nr, 2)), dma((2, nr)), dma((2, nr)),
            dma, dma((nc, n)), dma((n, n)), dma((nr, n, 2)), dma((nr, nc)), dma((nr, n, 2)), dma, dma((2, 2)), dma,
        ],
        compiler_params=pltpu.CompilerParams(
            collective_id=0, has_side_effects=True, vmem_limit_bytes=VMEM_BYTES,
        ),
    )(a, b, row_gap, col_gap)


def local(amplitudes, integrals, tile_mask, occ_energy, virt_energy):
    nr = lax.axis_size("row")
    nc = lax.axis_size("col")
    r = lax.axis_index("row")
    c = lax.axis_index("col")
    depth, width = amplitudes.shape
    tile_rows = depth // TILE
    tile_cols = width // TILE
    own_mask = lax.dynamic_slice_in_dim(tile_mask, c * tile_rows, tile_rows, 0)
    keep_tiles = own_mask.astype(jnp.bfloat16)
    keep = jnp.broadcast_to(keep_tiles[:, :, None], (tile_rows, tile_cols, TILE)).reshape(tile_rows, 1, width)
    masked = (amplitudes.reshape(tile_rows, TILE, width) * keep).reshape(depth, width)
    q = width // nc
    pair_gap = (virt_energy[None, :] - occ_energy[:, None]).reshape(-1)
    col_gap = lax.dynamic_slice_in_dim(pair_gap, r * width, width, 0)[None, :]
    row_gap = jnp.stack([lax.dynamic_slice_in_dim(pair_gap, (r ^ m) * width + c * q, q, 0) for m in range(nr)])
    return fused(nr, nc, masked, integrals, row_gap[:, :, None], col_gap)[0]


def solution(mesh):
    return jax.shard_map(
        local,
        mesh=mesh,
        in_specs=(P("col", "row"), P("row", "col"), P(None, "row"), P(), P()),
        out_specs=P(("row", "col"), None),
        check_vma=False,
    )
```

```python
import functools

import jax
import jax.numpy as jnp
from jax import lax
from jax.experimental import pallas as pl
from jax.experimental.pallas import tpu as pltpu
from jax.sharding import PartitionSpec as P

TILE = 64
MESH = pl.DeviceIdType.MESH
VMEM_BYTES = 66_000_000
DIMS = (((0,), (0,)), ((), ()))


def xor(u, v, n):
    total, bit = 0, 1
    while bit < n:
        total = total + (((u // bit) % 2 + (v // bit) % 2) % 2) * bit
        bit *= 2
    return total


def bits_of(n):
    out, bit = [], 1
    while bit < n:
        out.append(bit)
        bit *= 2
    return out


def children(m, parity, n):
    if m == 0:
        return bits_of(n)
    have = [b for b in bits_of(n) if m & b]
    if parity == 0:
        return [b for b in bits_of(n) if b < have[0]]
    return [b for b in bits_of(n) if b > have[-1]]


def after(k, n):
    odd = k % 2 == 1
    up = jnp.where(k + 2 <= n - 1, k + 2, n - 2)
    down = jnp.where(k == 0, 1, k - 2)
    return jnp.where(odd, up, down)


def before(k, n):
    odd = k % 2 == 1
    up = jnp.where(k + 2 <= n - 2, k + 2, n - 1)
    down = jnp.where(k == 1, 0, k - 2)
    return jnp.where(odd, down, up)


def kernel(
    nr, nc, a_ref, b_ref, rg_ref, cg_ref, out, a_full, ib,
    ra, rb, ca, cb, stage, twin,
    s_tr, s_own, s_fwd, s_part, s_ra, s_rb, s_bc, s_hand, s_rra, s_rrb, s_po, s_out, s_tw,
    q_tr, q_a, q_g, q_q, q_ra, q_rb, q_out, l_c, l_r,
):
    r = lax.axis_index("row")
    c = lax.axis_index("col")
    n = nc // 2
    k = c // 2
    p = c % 2
    partner = c + 1 - 2 * p
    d, w = a_ref.shape
    e = b_ref.shape[0]
    eh = e // 2
    sub = w // n
    q = sub // 2
    half = n // 2
    depth = d * nc
    nxt, prv = before(k, n), after(k, n)
    low = k < half
    top_skip, bottom_skip = n - 2, 1
    mirrored = jnp.where(low, k, n - 1 - k)
    end = mirrored == 0
    first = -1
    early = jnp.where(mirrored == 0, -1, n - 2 - mirrored)
    late = jnp.where(mirrored == 0, 0, mirrored + 1)
    bits = bits_of(nr)

    barrier = pltpu.get_barrier_semaphore()

    def greet(row, col):
        pl.semaphore_signal(barrier, inc=1, device_id=(row, col), device_id_type=MESH)

    greet(r, partner)
    for m in range(1, nr):
        greet(xor(r, m, nr), c)
        greet(xor(r, m, nr), partner)
    greet(r, (c + 2) % nc)
    greet(r, (c - 2 + nc) % nc)
    for t in range(2):
        greet(r, 2 * nxt + t)
        greet(r, 2 * prv + t)
    pl.semaphore_wait(barrier, 1 + 2 * (nr - 1) + 2 + 4)

    state = {"wait": False}

    def run(cond, body):
        if cond is None:
            body()
        else:
            pl.when(cond)(body)

    def both(*conds):
        total = None
        for x in conds:
            if x is None:
                continue
            total = x if total is None else jnp.logical_and(total, x)
        return total

    def no(x):
        return jnp.logical_not(x)

    def send(src, dst, sem, recv, row, col, cond=None):
        copy = pltpu.make_async_remote_copy(
            src_ref=src, dst_ref=dst, send_sem=sem, recv_sem=recv,
            device_id=(row, col), device_id_type=MESH,
        )
        run(cond, copy.wait_send if state["wait"] else copy.start)

    def local(src, dst, sem, cond=None):
        if not state["wait"]:
            run(cond, pltpu.make_async_copy(src, dst, sem).start)

    def arrived(ref, sem, cond=None):
        if not state["wait"]:
            run(cond, pltpu.make_async_copy(ref, ref, sem).wait)

    def ds(start, size):
        return pl.ds(pl.multiple_of(start, size), size)

    def a_rows(col):
        return ds(col * d, d)

    def b_rows(row):
        return ds(row * e, e)

    def cols(kp):
        return ds(kp * sub, sub)

    def h_rows(row, pp):
        return ds((2 * row + pp) * eh, eh)

    def raw(kk, kp, plane):
        direct = jnp.logical_and(kk == r, kp != plane)
        return ds(jnp.where(direct, 2 * r + p, 2 * nr + kk) * eh, eh)

    own = ds(c * q, q)

    def rows_a(src, col, cond):
        for x, b in enumerate(bits):
            send(src, ra.at[b, a_rows(col), :], s_ra.at[col, x], q_ra.at[b, col], xor(r, b, nr), c, cond)

    def b_out(src, kk, kp, cond):
        is_row = both(cond, kp == k)
        for t in range(2):
            part = src.at[:, pl.ds(t * q, q)]
            for x, b in enumerate(bits):
                row = xor(r, b, nr)
                send(
                    part, rb.at[xor(row, kk, nr), h_rows(r, p), :], s_rb.at[kk, t, x], q_rb.at[b, kk, p],
                    row, 2 * k + t, is_row,
                )
            dst = rb.at[xor(r, kk, nr), h_rows(r, p), :]
            local(part, dst, q_rb.at[0, kk, p], both(is_row, p == t))
            send(part, dst, s_rb.at[kk, t, len(bits)], q_rb.at[0, kk, p], r, partner, both(is_row, p != t))

    def spread(src, kk, kp, cond):
        ok = both(cond, kp != k, kp != prv)
        dst = ib.at[h_rows(r, p), cols(kp)]
        send(src, dst, s_bc.at[kk, kp], q_q.at[r, kp, p], kk, c, both(ok, kk != r))
        send(src, dst, s_bc.at[kk, kp], q_q.at[r, kp, p], r, partner, both(ok, kk == r))

    def mine_of(kp):
        return (
            (b_ref.at[ds(p * eh, eh), cols(kp % half)], owner(kp)),
            (ib.at[ds((2 * nr + k) * eh, eh), cols(kp)], no(owner(kp))),
        )

    def trade():
        other = 1 - p
        dst = ib.at[ds((2 * nr + k) * eh, eh), ds(p * (w // 2), w // 2)]
        send(b_ref.at[ds(other * eh, eh), :], dst, s_tr, q_tr, r, partner)
        arrived(dst, q_tr)

    def blocked(target, kp):
        return jnp.logical_or(
            jnp.logical_and(target == 0, kp == bottom_skip),
            jnp.logical_and(target == n - 1, kp == top_skip),
        )

    def owner(kp):
        return kp // half == p

    def piece(sign, j):
        return jnp.where(sign > 0, n - 1 - j, j)

    def swap(j):
        return jnp.where(j == 1, 2, jnp.where(j == 2, 1, j))

    def edge(sign):
        return jnp.where(sign > 0, 0, n - 1)

    def valid(j):
        return jnp.logical_and(j >= 0, j < n)

    def clip(x, top):
        return jnp.clip(x, 0, top)

    def issue_own(sign, j, when=None):
        ok = both(valid(j), when)
        kp = piece(sign, jnp.where(k == edge(sign), swap(clip(j, n - 1)), clip(j, n - 1)))
        far = k + sign
        ok = both(ok, far >= 0, far < n, no(blocked(far, kp)))
        x = jnp.where(sign > 0, 0, 1)
        target = clip(c + 2 * sign, nc - 1)
        send(a_ref.at[:, cols(kp)], a_full.at[a_rows(c), cols(kp)], s_own.at[x, 0, kp], q_a.at[c, kp], r, target, ok)
        for src, cond in mine_of(kp):
            send(
                src, ib.at[raw(k, kp, far), cols(kp)], s_own.at[x, 1, kp], q_g.at[k, kp],
                r, target, both(ok, cond),
            )

    def order(sign, j, s, src):
        j = clip(j, n - 1)
        return piece(sign, jnp.where(src == edge(sign), swap(j), j) if s == 1 else j)

    def relay(sign, j, s, tau, go, hold):
        src = jnp.where(go, k - sign * s, -1)
        kp = order(sign, j, s, src)
        here = both(valid(j), src >= 0, src < n, no(blocked(k, kp)))
        kk = clip(src, n - 1)
        far = k + sign
        x = jnp.where(sign > 0, 0, 1)
        target = clip(c + 2 * sign, nc - 1)
        col = 2 * kk + p

        def onward(which, kp, cond):
            ok = both(cond, valid(j), src >= 0, src < n, far >= 0, far < n, no(blocked(far, kp)))
            if which == 0:
                ref = a_full.at[a_rows(col), cols(kp)]
                send(ref, ref, s_fwd.at[x, s - 1, 0, kp], q_a.at[col, kp], r, target, ok)
            else:
                send(
                    ib.at[raw(kk, kp, k), cols(kp)], ib.at[raw(kk, kp, far), cols(kp)],
                    s_fwd.at[x, s - 1, 1, kp], q_g.at[kk, kp], r, target, ok,
                )

        held = both(src == edge(sign), j == 1) if s == 1 else None
        freed = both(src == edge(sign), j == 2)
        a_piece = a_full.at[a_rows(col), cols(kp)]
        arrived(a_piece, q_a.at[col, kp], here)
        onward(0, kp, no(held) if s == 1 else None)
        send(a_piece, a_piece, s_part.at[kk, kp], q_a.at[col, kp], r, partner, both(here, kp != prv))
        rows_a(a_full.at[a_rows(col), own], col, both(here, kp == k))
        b_piece = ib.at[raw(kk, kp, k), cols(kp)]
        arrived(b_piece, q_g.at[kk, kp], here)
        onward(1, kp, no(held) if s == 1 else None)
        last = both(valid(j), src == edge(sign))
        if s == 1:
            issue_own(sign, 2, freed)
            onward(0, order(sign, 1, 1, src), freed)
            onward(1, order(sign, 1, 1, src), freed)
            issue_own(sign, j + 1, both(last, j != 1))
        else:
            issue_own(sign, j + jnp.where(far == edge(-sign), 2, 1), last)
        b_out(b_piece, kk, kp, here)
        spread(b_piece, kk, kp, both(here, tau > late, None if hold is None else no(hold)))

    def partner_rows(kk, cond):
        col = 2 * kk + 1 - p
        ref = a_full.at[a_rows(col), cols(k)]
        arrived(ref, q_a.at[col, k], cond)
        rows_a(a_full.at[a_rows(col), own], col, cond)

    def own_part():
        rows_a(a_ref.at[:, own], c, None)

        @pl.loop(0, n)
        def _(kp):
            for src, cond in mine_of(kp):
                b_out(src, k, kp, cond)
                local(src, ib.at[h_rows(r, p), cols(kp)], q_q.at[r, kp, p], both(cond, k == r, kp != k, kp != prv))
            part = a_ref.at[:, cols(kp)]
            dst = a_full.at[a_rows(c), cols(kp)]
            send(part, dst, s_part.at[k, kp], q_a.at[c, kp], r, partner, kp != prv)
            local(part, dst, q_a.at[c, kp], kp != prv)

    def slot(tau, lo=1, hi=None, hold=None):
        lag = jnp.where(low, -1, 1)
        ways = ((lag, tau), (-lag, tau + 1))
        hi = n - 1 if hi is None else hi
        for s in range(1, n):
            go = jnp.logical_and(s >= lo, s <= hi)
            for sign, j in ways:
                relay(sign, j, s, tau, go, hold)
        for s in range(1, n):
            go = jnp.logical_and(s >= lo, s <= hi)
            for sign, j in ways:
                src = jnp.where(go, k - sign * s, -1)
                cond = both(valid(j), src >= 0, src < n, order(sign, j, s, src) == k)
                partner_rows(clip(src, n - 1), cond)

    def pass_rows(kk, m, cond):
        origin = xor(r, m, nr)
        for pp in range(2):
            if m:
                col = 2 * kk + pp
                got = ra.at[m, a_rows(col), :]
                arrived(got, q_ra.at[m, col], cond)
                for b in children(m, pp, nr):
                    x = bits.index(b)
                    send(
                        got, ra.at[m | b, a_rows(col), :], s_rra.at[col, m, x], q_ra.at[m | b, col],
                        xor(r, b, nr), c, cond,
                    )
            got = rb.at[xor(r, kk, nr), h_rows(origin, pp), :]
            arrived(got, q_rb.at[m, kk, pp], cond)
            if m:
                for b in children(m, pp, nr):
                    x = bits.index(b)
                    row = xor(r, b, nr)
                    send(
                        got, rb.at[xor(row, kk, nr), h_rows(origin, pp), :], s_rrb.at[kk, m, pp, x],
                        q_rb.at[m | b, kk, pp], row, c, cond,
                    )
            dst = ib.at[h_rows(origin, pp), own]
            send(got, dst, s_po.at[m, pp], q_q.at[origin, k, pp], r, partner, both(cond, kk == r))

    def pass_direct(tau):
        @pl.loop(0, n)
        def _(kk):
            away = jnp.abs(kk - k)
            lag = jnp.where(away == 1, mirrored, late)
            near = jnp.where((kk < k) == low, early, lag)
            when = jnp.where(kk == k, first, near)
            for m in bits:
                pass_rows(kk, m, tau == when)

    def pass_rest():
        @pl.loop(0, n)
        def _(kk):
            for m in range(nr):
                if m not in bits:
                    pass_rows(kk, m, None)

    def spread_all(go, held=False):
        @pl.loop(0, n)
        def _(kp):
            for m in [*range(1, nr), 0]:
                kk = xor(r, m, nr)
                up = jnp.where(jnp.logical_and(kk == 0, k == 1), swap(n - 1 - kp), n - 1 - kp)
                down = jnp.where(jnp.logical_and(kk == n - 1, k == n - 2), swap(kp), kp)
                came = jnp.where(kk < k, up - jnp.where(low, 1, 0), down - jnp.where(low, 0, 1))
                ok = both(go, no(blocked(k, kp)))
                for src, cond in mine_of(kp):
                    spread(src, kk, kp, both(ok, kk == k, cond))
                there = ib.at[raw(kk, kp, k), cols(kp)]
                ready = came <= late
                if held:
                    away = jnp.abs(kk - k)
                    ready = jnp.logical_or(ready, jnp.logical_or(away == 1, jnp.logical_and(away == 2, came == 2)))
                spread(there, kk, kp, both(ok, kk != k, ready))

    def hand(kp, cond):
        for m in range(nr):
            row = xor(r, m, nr)
            ref = ib.at[h_rows(row, p), cols(kp)]
            if m:
                arrived(ref, q_q.at[row, kp, p], cond)
                send(ref, ref, s_hand.at[row, kp], q_q.at[row, kp, p], r, partner, cond)
            else:
                arrived(ref, q_q.at[row, kp, p], both(cond, k == r))

    def tile_piece(t):
        rank = jnp.where(low, prv, n - 1 - prv)
        base = jnp.where(mirrored < rank, mirrored, mirrored - 1)
        i = jnp.where(t == 0, base, jnp.where(t <= base, t - 1, t))
        i = jnp.where(i >= rank, i + 1, i)
        return jnp.where(low, i, n - 1 - i)

    def tile(t):
        kp = tile_piece(t)
        is_own = kp == k
        for kk in range(n):
            col = 2 * kk + 1 - p
            arrived(a_full.at[a_rows(col), cols(kp)], q_a.at[col, kp], no(is_own))
        arrived(a_full.at[a_rows(c), cols(kp)], q_a.at[c, kp], no(is_own))
        for row in range(nr):
            arrived(ib.at[h_rows(row, 1 - p), cols(kp)], q_q.at[row, kp, 1 - p], no(is_own))
            for pp in range(2):
                arrived(ib.at[h_rows(row, pp), own], q_q.at[row, k, pp], is_own)

        def load(h):
            where = ds((2 * kp + h) * q, q)
            full = pl.ds(0, depth)
            pltpu.make_async_copy(a_full.at[:, where], ca.at[h], l_c.at[h, 0]).start()
            mine = jnp.logical_and(is_own, p == h)
            run(mine, pltpu.make_async_copy(rb.at[0], cb.at[h], l_c.at[h, 1]).start)
            run(no(mine), pltpu.make_async_copy(ib.at[full, where], cb.at[h], l_c.at[h, 1]).start)

        for h in range(2):
            load(h)

        @pl.loop(0, 2)
        def _(h):
            pl.when(both(end, h == 1, t > 0, t + 2 < n))(functools.partial(slot, t + 2, 3))
            where = ds((2 * kp + h) * q, q)
            pltpu.make_async_copy(ca.at[h], ca.at[h], l_c.at[h, 0]).wait()
            pltpu.make_async_copy(cb.at[h], cb.at[h], l_c.at[h, 1]).wait()

            @pl.loop(0, nr)
            def _(i):
                m = nr - 1 - i
                row = xor(r, m, nr)
                buf = stage.at[h, m]
                run(t > 0, pltpu.make_async_copy(buf, buf, s_out.at[h, m]).wait)
                total = lax.dot_general(ra[m], cb[h], DIMS, preferred_element_type=jnp.float32)
                total += lax.dot_general(rb[m], ca[h], DIMS, preferred_element_type=jnp.float32)
                total = total / (rg_ref[m] + cg_ref[:, where])
                stage[h, m] = total.astype(stage.dtype)
                dst = out.at[:, ds(r * w + (2 * kp + h) * q, q)]
                remote = pltpu.make_async_remote_copy(
                    src_ref=buf, dst_ref=dst, send_sem=s_out.at[h, m], recv_sem=q_out,
                    device_id=(row, c), device_id_type=MESH,
                )
                run(m > 0, remote.start)
                run(m == 0, pltpu.make_async_copy(buf, dst, s_out.at[h, m]).start)

                @pl.when(kp == nxt)
                def _():
                    twin[h, m] = total.T.astype(twin.dtype)
                    pltpu.make_async_remote_copy(
                        src_ref=twin.at[h, m], dst_ref=out.at[:, ds(row * w + c * q, q)],
                        send_sem=s_tw.at[h, m], recv_sem=q_out,
                        device_id=(r, 2 * kp + h), device_id_type=MESH,
                    ).start()


    def start():
        trade()
        for sign in (1, -1):
            for j in range(n):
                issue_own(jnp.int32(sign), jnp.int32(j), None if j == 0 else k == edge(sign))
        own_part()
        partner_rows(k, None)

    start()

    @pl.loop(0, n + 3)
    def _(x):
        i = x - 3
        ahead = jnp.logical_and(end, i >= 0)
        final = i == n - 2
        first_part = jnp.logical_and(no(end), x - 2 == late)
        second_part = jnp.logical_and(no(end), x - 2 == late + 1)
        plain = jnp.where(jnp.logical_or(end, x - 2 <= late), x - 2, x - 3)
        closing = jnp.logical_and(no(end), x == n + 2)
        tau = jnp.where(ahead, jnp.where(final, 2, i + 2), plain)
        lo = jnp.where(jnp.logical_or(jnp.logical_and(ahead, final), second_part), 2, 1)
        top = jnp.where(jnp.logical_or(first_part, closing), 1, n - 1)
        hi = jnp.where(ahead, jnp.where(i > n - 2, 0, lo), top)
        slot(tau, lo, hi, end)
        pass_direct(jnp.where(jnp.logical_or(ahead, second_part), n, plain))
        spread_all(both(no(end), no(first_part), plain == late))

    pass_rest()
    arrived(a_full.at[a_rows(c), cols(k)], q_a.at[c, k])
    load_own = pltpu.make_async_copy(a_full.at[:, own], ra.at[0], l_r)
    load_own.start()
    load_own.wait()
    spread_all(end, True)

    @pl.loop(0, jnp.where(end, n, n - 1))
    def _(x):
        @pl.when(jnp.logical_or(jnp.logical_and(end, jnp.logical_and(x > 0, x < n - 1)), jnp.logical_and(no(end), x == 1)))
        def _():
            slot(
                jnp.where(end, x + 1, n - 1), jnp.where(jnp.logical_and(end, x == 1), 3, 2),
                jnp.where(jnp.logical_and(end, x > 1), 2, n - 1),
            )

        @pl.when(no(jnp.logical_and(end, x == 1)))
        def _():
            t = jnp.where(jnp.logical_and(end, x > 1), x - 1, x)
            hand(tile_piece(t), t > 0)
            tile(t)

    state["wait"] = True
    start()

    @pl.loop(0, n + 2)
    def _(x):
        slot(x - 2)
        pass_direct(x - 2)
        spread_all(x - 2 == late)

    pass_rest()

    @pl.loop(1, n - 1)
    def _(t):
        hand(tile_piece(t), None)

    @pl.loop(0, 2)
    def _(h):
        @pl.loop(0, nr)
        def _(m):
            pltpu.make_async_copy(stage.at[h, m], stage.at[h, m], s_out.at[h, m]).wait()
            pltpu.make_async_copy(twin.at[h, m], twin.at[h, m], s_tw.at[h, m]).wait()

    landed = out.at[:, pl.ds(0, (nr - 1) * (n - 1) * sub + nr * sub)]
    pltpu.make_async_copy(landed, landed, q_out).wait()


def fused(nr, nc, a, b, row_gap, col_gap):
    d, w = a.shape
    e = b.shape[0]
    n = nc // 2
    depth = d * nc
    q = w // nc
    nb = len(bits_of(nr))
    dma = pltpu.SemaphoreType.DMA
    hbm = pl.BlockSpec(memory_space=pl.ANY)
    vmem = pl.BlockSpec(memory_space=pltpu.VMEM)
    shapes = [(q, nr * w), (depth, w), (nr * e + n * e // 2, w)]
    block = pltpu.VMEM((nr, depth, q), a.dtype)
    pair = pltpu.VMEM((2, depth, q), a.dtype)
    tiles = pltpu.VMEM((2, nr, q, q), a.dtype)
    return pl.pallas_call(
        functools.partial(kernel, nr, nc),
        out_shape=[jax.ShapeDtypeStruct(s, a.dtype) for s in shapes],
        in_specs=[hbm, hbm, vmem, vmem],
        out_specs=[hbm] * 3,
        scratch_shapes=[
            block, block, pair, pair, tiles, tiles,
            dma, dma((2, 2, n)), dma((2, n - 1, 2, n)), dma((n, n)), dma((nc, nb)), dma((n, 2, nb + 1)),
            dma((n, n)), dma((nr, n)), dma((nc, nr, nb)), dma((n, nr, 2, nb)), dma((nr, 2)), dma((2, nr)), dma((2, nr)),
            dma, dma((nc, n)), dma((n, n)), dma((nr, n, 2)), dma((nr, nc)), dma((nr, n, 2)), dma, dma((2, 2)), dma,
        ],
        compiler_params=pltpu.CompilerParams(
            collective_id=0, has_side_effects=True, vmem_limit_bytes=VMEM_BYTES,
        ),
    )(a, b, row_gap, col_gap)


def local(amplitudes, integrals, tile_mask, occ_energy, virt_energy):
    nr = lax.axis_size("row")
    nc = lax.axis_size("col")
    r = lax.axis_index("row")
    c = lax.axis_index("col")
    depth, width = amplitudes.shape
    tile_rows = depth // TILE
    tile_cols = width // TILE
    own_mask = lax.dynamic_slice_in_dim(tile_mask, c * tile_rows, tile_rows, 0)
    keep_tiles = own_mask.astype(jnp.bfloat16)
    keep = jnp.broadcast_to(keep_tiles[:, :, None], (tile_rows, tile_cols, TILE)).reshape(tile_rows, 1, width)
    masked = (amplitudes.reshape(tile_rows, TILE, width) * keep).reshape(depth, width)
    q = width // nc
    pair_gap = (virt_energy[None, :] - occ_energy[:, None]).reshape(-1)
    col_gap = lax.dynamic_slice_in_dim(pair_gap, r * width, width, 0)[None, :]
    row_gap = jnp.stack([lax.dynamic_slice_in_dim(pair_gap, (r ^ m) * width + c * q, q, 0) for m in range(nr)])
    return fused(nr, nc, masked, integrals, row_gap[:, :, None], col_gap)[0]


def solution(mesh):
    return jax.shard_map(
        local,
        mesh=mesh,
        in_specs=(P("col", "row"), P("row", "col"), P(None, "row"), P(), P()),
        out_specs=P(("row", "col"), None),
        check_vma=False,
    )
```
